32 devices in a mesh: expert: 8 (over z, core), fsdp: 4 (over y, x).
Axes of the slice: x: 2, y: 2, z: 4, core: 2. Of those that a mesh axis runs over, the one named last changes fastest.
Arguments:
- hidden_in: bfloat16 [16384, 768], P(('expert', 'fsdp')), may hold values from -6 to 6
- routes: int32 [16384, 2], P(('expert', 'fsdp')), may hold values from 0 to 7, all different within a row; in each aligned block of 512 rows (0 to 511, 512 to 1023, ...) at most 256 rows name the same one
- attn_gain: bfloat16 [768], P(('expert', 'fsdp')), may hold values from 0.25 to 1.75
- w_query: bfloat16 [768, 768], P(('expert', 'fsdp')), may hold values from -0.21875 to 0.21875
- w_key: bfloat16 [768, 768], P(('expert', 'fsdp')), may hold values from -0.21875 to 0.21875
- w_value: bfloat16 [768, 768], P(('expert', 'fsdp')), may hold values from -0.21875 to 0.21875
- w_output: bfloat16 [768, 768], P(('expert', 'fsdp')), may hold values from -1.25 to 1.25
- ffn_gain: bfloat16 [768], P(('expert', 'fsdp')), may hold values from 0.25 to 1.75
- w_router: bfloat16 [768, 8], P(('expert', 'fsdp')), may hold values from -0.21875 to 0.21875
- shared_gate: bfloat16 [768, 2048], P(('expert', 'fsdp')), may hold values from -0.21875 to 0.21875
- shared_up: bfloat16 [768, 2048], P(('expert', 'fsdp')), may hold values from -0.21875 to 0.21875
- shared_down: bfloat16 [2048, 768], P(('expert', 'fsdp')), may hold values from -0.125 to 0.125
- expert_gate: bfloat16 [8, 768, 2048], P('expert', 'fsdp'), may hold values from -0.21875 to 0.21875
- expert_up: bfloat16 [8, 768, 2048], P('expert', 'fsdp'), may hold values from -0.21875 to 0.21875
- expert_down: bfloat16 [8, 2048, 768], P('expert', 'fsdp'), may hold values from -0.125 to 0.125
- cotangent: bfloat16 [16384, 768], P(('expert', 'fsdp')), may hold values from -6 to 6
Outputs:
- hidden_out: bfloat16 [16384, 768], P(('expert', 'fsdp'))
- grad_hidden: float32 [16384, 768], P(('expert', 'fsdp'))
- grad_attn_gain: float32 [768], P(('expert', 'fsdp'))
- grad_query: float32 [768, 768], P(('expert', 'fsdp'))
- grad_key: float32 [768, 768], P(('expert', 'fsdp'))
- grad_value: float32 [768, 768], P(('expert', 'fsdp'))
- grad_output: float32 [768, 768], P(('expert', 'fsdp'))
- grad_ffn_gain: float32 [768], P(('expert', 'fsdp'))
- grad_router: float32 [768, 8], P(('expert', 'fsdp'))
- grad_shared_gate: float32 [768, 2048], P(('expert', 'fsdp'))
- grad_shared_up: float32 [768, 2048], P(('expert', 'fsdp'))
- grad_shared_down: float32 [2048, 768], P(('expert', 'fsdp'))
- grad_expert_gate: float32 [8, 768, 2048], P('expert', 'fsdp')
- expert_up_weight_gradient: float32 [8, 768, 2048], P('expert', 'fsdp')
- grad_expert_down: float32 [8, 2048, 768], P('expert', 'fsdp')
The draws below stay inside these ranges and needn't reach their ends.
Inputs may be any that keep to these rules, and one draw needn't show every extreme that they name: `routes`: each row names 2 different experts. In the rows of one device no expert is named more than 256 times, and in every draw some device's rows name some expert exactly 256 times.
All inputs are finite; a program needn't handle non-finite values.
Results may differ from the reference program's by a relative error of at most 0.015.
Values may be sent and summed in bfloat16 or wider, within the bound.
No kernel may reach another device: no remote copies, remote signals or barrier semaphores. Data moves between devices by JAX's collectives and lax.ppermute only.
A program may use at most 256 MiB of HBM per device.

```python
import math
import jax
import jax.numpy as jnp
import numpy as np
from jax import lax

D = 768
HEADS = 12
HEAD_DIM = 64
F = 2048
FS = 2048
TOP = 2
BLOCK = 256
TOK_DEV = 512
EXPERTS = 8
CAP = 256
TOKENS = 16384


def with_spikes(drawn, own_key, source, target, blocks, factor):
    owner, partner = [(jnp.arange(drawn.shape[axis_at]) // (drawn.shape[axis_at] // blocks)).reshape([-1 if axis == axis_at else 1 for axis in range(drawn.ndim)]) for axis_at in (source, target)]
    chosen = jax.random.permutation(own_key, blocks)[partner]
    strong = (owner == chosen) | (owner == (partner + blocks // 2) % blocks)
    return jnp.where(strong, factor * drawn, drawn)


def shard_levels(own_key, dims, cuts, smallest, largest):
    factor_of = 1.0
    for dim, blocks in cuts:
        heights = jax.random.uniform(jax.random.fold_in(jax.random.fold_in(own_key, 6), dim), (blocks,), jnp.float32, smallest / len(cuts), largest / len(cuts))
        factor_of = factor_of * jnp.repeat(jnp.exp(heights), dims[dim] // blocks).reshape((-1,) + (1,) * (len(dims) - 1 - dim))
    return factor_of


def shared_out(rng, own, number, rows, count, top, limit, skew):
    order = jax.random.permutation(rng, count)
    crowded, usual = portions_of(count, rows * top, limit, skew, True), portions_of(count, rows * top, limit, skew, False)
    places = jnp.arange(count)

    def named(tallies, turn):
        used = int((tallies > 0).sum())
        fixed = max(1, used // 4)
        shifted = fixed + (places - fixed + turn * (used - fixed)) % max(1, count - fixed)
        return jnp.zeros((count,), jnp.int32).at[order[jnp.where(places < fixed, places, shifted)]].set(jnp.asarray(tallies, jnp.int32))

    tallies = jnp.where(number % 4 == 0, named(crowded, number // 4), named(usual, number - number // 4 - 1))
    mixed = jax.random.permutation(jax.random.fold_in(own, 3), count)
    donor, taker = mixed[0:count // 2 * 2:2], mixed[1:count // 2 * 2:2]
    slack = jnp.minimum(tallies[donor] - 1, limit - tallies[taker]) // 2
    slack = jnp.where((donor == order[0]) | (taker == order[0]) | (tallies[taker] == 0), 0, jnp.maximum(slack, 0))
    shifted = jax.random.randint(jax.random.fold_in(own, 4), (count // 2,), 0, 1 << 20) % (slack + 1)
    tallies = tallies.at[donor].add(-shifted).at[taker].add(shifted)
    items = jnp.searchsorted(jnp.cumsum(tallies), jnp.arange(rows * top), side="right").astype(jnp.int32)
    listing = items.reshape(top, rows).T
    listing = listing[jax.random.permutation(jax.random.fold_in(own, 1), rows)]
    turn = jax.random.randint(jax.random.fold_in(own, 2), (rows, 1), 0, top)
    return jnp.take_along_axis(listing, (jnp.arange(top)[None, :] + turn) % top, axis=1)


def portions_of(amount, total, bound, skew, full):
    loads = [(1 << 20) // math.isqrt(rank ** skew) + 1 for rank in range(1, amount + 1)]
    largest = bound if full else min(bound, max(-(-total // amount), total * loads[0] // sum(loads)))
    least = 1 if total - largest >= amount - 1 else 0
    holding, spare = [largest] + [least] * (amount - 1), total - largest - least * (amount - 1)
    while spare > 0:
        movable = [i for i in range(1, amount) if holding[i] < largest] or [i for i in range(1, amount) if holding[i] < bound]
        pool, budget = sum([loads[i] for i in movable]), spare
        for i in movable:
            more = min(bound - holding[i], max(1, budget * loads[i] // pool), spare)
            holding[i] = holding[i] + more
            spare = spare - more
    return np.array(holding)


def gaussian(own_key, extent, width, reach, pieces=(), kind=jnp.bfloat16):
    factor_of = shard_levels(own_key, extent, pieces, -0.22, 0.18) if pieces else 1.0
    array = jax.random.normal(own_key, extent, jnp.float32) * width * factor_of
    return jnp.minimum(jnp.maximum(array, -reach), reach).astype(kind)


def gaussian_with(stream_key, dims, spread, bound, cuts, heavy, held_as=jnp.bfloat16):
    values = spread * jax.random.normal(stream_key, dims, jnp.float32)
    if cuts:
        values = values * shard_levels(stream_key, dims, cuts, -0.22, 0.18)
    return jnp.clip(with_spikes(values, jax.random.fold_in(stream_key, 3), *heavy), -bound, bound).astype(held_as)


def setup_inputs(seed: int = 0) -> dict:
    seeds = jax.random.split(jax.random.key(seed), 17)
    hidden_in = gaussian_with(seeds[0], (TOKENS, D), 1.0, 6.0, ((0, 32),), (0, 1, 32, 2.75))
    routes_keys = jax.random.split(jax.random.fold_in(seeds[1], 1), TOKENS // TOK_DEV)
    routes_turns = jax.random.permutation(jax.random.fold_in(seeds[1], 3), TOKENS // TOK_DEV)
    routes = jax.vmap(lambda own, number: shared_out(jax.random.fold_in(seeds[1], 2), own, number, TOK_DEV, EXPERTS, TOP, CAP, 2))(routes_keys, routes_turns).reshape((TOKENS, TOP))
    attn_gain = jnp.clip(1.0 + 0.15 * jax.random.normal(seeds[2], (D,), jnp.float32), 0.25, 1.75).astype(jnp.bfloat16)
    w_query = gaussian(seeds[3], (D, D), D ** -0.5, 0.21875, ((0, 32),))
    w_key = gaussian(seeds[4], (D, D), D ** -0.5, 0.21875, ((0, 32),))
    w_value = gaussian(seeds[5], (D, D), D ** -0.5, 0.21875, ((0, 32),))
    w_output = gaussian(seeds[6], (D, D), (D // 32) ** -0.5, 1.25, ((0, 32),))
    ffn_gain = jnp.clip(1.0 + 0.15 * jax.random.normal(seeds[7], (D,), jnp.float32), 0.25, 1.75).astype(jnp.bfloat16)
    w_router = gaussian(seeds[8], (D, EXPERTS), D ** -0.5, 0.21875, ((0, 32),))
    shared_gate = gaussian(seeds[9], (D, FS), D ** -0.5, 0.21875, ((0, 32),))
    shared_up = gaussian(seeds[10], (D, FS), D ** -0.5, 0.21875, ((0, 32),))
    shared_down = gaussian(seeds[11], (FS, D), FS ** -0.5, 0.125, ((0, 32),))
    expert_gate = gaussian(seeds[12], (EXPERTS, D, F), D ** -0.5, 0.21875, ((0, 8), (1, 4)))
    expert_up = gaussian(seeds[13], (EXPERTS, D, F), D ** -0.5, 0.21875, ((0, 8), (1, 4)))
    expert_down = gaussian(seeds[14], (EXPERTS, F, D), F ** -0.5, 0.125, ((0, 8), (1, 4)))
    cotangent = gaussian(seeds[15], (TOKENS, D), 1.0, 6.0, ((0, 32),))
    return dict(hidden_in=hidden_in, routes=routes, attn_gain=attn_gain, w_query=w_query, w_key=w_key, w_value=w_value, w_output=w_output, ffn_gain=ffn_gain, w_router=w_router, shared_gate=shared_gate, shared_up=shared_up, shared_down=shared_down, expert_gate=expert_gate, expert_up=expert_up, expert_down=expert_down, cotangent=cotangent)


EPSILON = 1e-06
NEGATIVE = -1e+30
HIGHEST = lax.Precision.HIGHEST

@jax.custom_vjp
def low(v):
    return lax.optimization_barrier(v.astype(jnp.bfloat16)).astype(jnp.float32)

@jax.custom_vjp
def low_back(v):
    return v

def low_keep(v):
    return (low(v), None)

def low_pass(kept, grad):
    return (grad,)

def back_keep(v):
    return (v, None)

def back_low(kept, grad):
    return (low(grad),)
low.defvjp(low_keep, low_pass)
low_back.defvjp(back_keep, back_low)

def matmul(left, right):
    return jnp.dot(left, right, precision=HIGHEST, preferred_element_type=jnp.float32)

def rms_scale(values, gain):
    return values * lax.rsqrt(lax.optimization_barrier(jnp.mean(values * values, axis=-1, keepdims=True)) + EPSILON) * gain

def rope_tables(length, head_size):
    half = head_size // 2
    freqs = jnp.exp(-jnp.log(10000.0) * jnp.arange(half, dtype=jnp.float32) * 2.0 / head_size)
    angles = jnp.arange(length, dtype=jnp.float32)[:, None] * freqs[None, :]
    return (jnp.cos(angles)[:, None, :], jnp.sin(angles)[:, None, :])

def rotate(values, cosine, sine):
    half = values.shape[-1] // 2
    first = values[..., :half]
    second = values[..., half:]
    return jnp.concatenate([first * cosine - second * sine, second * cosine + first * sine], axis=-1)

def attend(normed, query_weight, key_weight, value_weight, output_weight, cosine, sine, allowed):
    length = normed.shape[0]
    query_raw = low_back(matmul(normed, query_weight)).reshape(length, HEADS, HEAD_DIM)
    query_states = low(rotate(query_raw, cosine, sine))
    key_raw = low_back(matmul(normed, key_weight)).reshape(length, HEADS, HEAD_DIM)
    key_states = low(rotate(key_raw, cosine, sine))
    value_states = low(low_back(matmul(normed, value_weight))).reshape(length, HEADS, HEAD_DIM)
    scores = low_back(jnp.einsum('qhd,khd->hqk', query_states, key_states, precision=HIGHEST) * HEAD_DIM ** (-0.5))
    probability = jax.nn.softmax(jnp.where(allowed[None], scores, NEGATIVE), axis=-1)
    mixture = jnp.einsum('hqk,khd->qhd', low(probability), value_states, precision=HIGHEST).reshape(length, HEADS * HEAD_DIM)
    mixture = low(low_back(mixture))
    return low_back(matmul(mixture, output_weight))

def slot_index(route_rows):
    flat = route_rows.reshape(-1)
    onehot = (flat[:, None] == jnp.arange(EXPERTS, dtype=jnp.int32)[None, :]).astype(jnp.int32)
    place = lax.optimization_barrier(jnp.sum((jnp.cumsum(onehot, axis=0) - onehot) * onehot, axis=1))
    return (flat * CAP + place).astype(jnp.int32)

def fill_slots(slot_row, copy_rows):
    return jnp.zeros((EXPERTS * CAP, D), jnp.float32).at[slot_row].set(copy_rows)

def take_rows(result_rows, slot_row):
    return result_rows[slot_row]

def layer_group(group_rows, group_routes, params):
    gain_one, query_weight, key_weight, value_weight, output_weight, gain_two, router_weight, shared_gating, shared_upward, shared_downward, expert_gate_activation, expert_up_projection, expert_downward = params
    group_size = group_rows.shape[0]
    cosine, sine = rope_tables(TOK_DEV, HEAD_DIM)
    block_ids = jnp.arange(TOK_DEV, dtype=jnp.int32) // BLOCK
    allowed = block_ids[None, :] <= block_ids[:, None]

    def attend_one(normed):
        return attend(normed, query_weight, key_weight, value_weight, output_weight, cosine, sine, allowed)
    normed_first = low(rms_scale(group_rows, gain_one))
    after_attn = group_rows + jax.vmap(attend_one)(normed_first)
    normed_second = low(rms_scale(after_attn, gain_two))
    logits = low_back(jnp.einsum('gtd,de->gte', normed_second, router_weight, precision=HIGHEST))
    chosen = jnp.take_along_axis(logits, group_routes, axis=2)
    gates = jax.nn.softmax(chosen, axis=-1)
    slots = jax.vmap(slot_index)(group_routes)
    copies = jnp.stack([low_back(normed_second) for route_index in range(TOP)], axis=2)
    copies = copies.reshape(group_size, TOK_DEV * TOP, D)
    buffers = jax.vmap(fill_slots)(slots, copies)
    grouped = buffers.reshape(group_size, EXPERTS, CAP, D).transpose(1, 0, 2, 3).reshape(EXPERTS, group_size * CAP, D)
    gate_part = low_back(jnp.einsum('erd,edf->erf', grouped, expert_gate_activation, precision=HIGHEST))
    up_part = low_back(jnp.einsum('erd,edf->erf', grouped, expert_up_projection, precision=HIGHEST))
    inner = low(jax.nn.silu(gate_part) * up_part)
    result = low(low_back(jnp.einsum('erf,efd->erd', inner, expert_downward, precision=HIGHEST)))
    result = result.reshape(EXPERTS, group_size, CAP, D).transpose(1, 0, 2, 3).reshape(group_size, EXPERTS * CAP, D)
    picked = jax.vmap(take_rows)(result, slots).reshape(group_size, TOK_DEV, TOP, D)
    routed = jnp.einsum('gtj,gtjd->gtd', gates, picked, precision=HIGHEST)
    shared_gate_part = low_back(jnp.einsum('gtd,df->gtf', normed_second, shared_gating, precision=HIGHEST))
    shared_up_part = low_back(jnp.einsum('gtd,df->gtf', normed_second, shared_upward, precision=HIGHEST))
    shared_inner = low(jax.nn.silu(shared_gate_part) * shared_up_part)
    shared_result = low_back(jnp.einsum('gtf,fd->gtd', shared_inner, shared_downward, precision=HIGHEST))
    return after_attn + routed + shared_result

def forward(flat, routes, params):
    blocks = TOKENS // TOK_DEV
    group_size = math.gcd(blocks, max(1, 4096 // TOK_DEV))
    group_count = blocks // group_size
    stacked = flat.reshape(group_count, group_size, TOK_DEV, D)
    route_groups = routes.reshape(group_count, group_size, TOK_DEV, TOP)

    def one_group(operands):
        return layer_group(operands[0], operands[1], params)
    result = lax.map(jax.checkpoint(one_group), (stacked, route_groups))
    return result.reshape(TOKENS, D)

def reference(hidden_in, routes, attn_gain, w_query, w_key, w_value, w_output, ffn_gain, w_router, shared_gate, shared_up, shared_down, expert_gate, expert_up, expert_down, cotangent):
    params = tuple((item.astype(jnp.float32) for item in (attn_gain, w_query, w_key, w_value, w_output, ffn_gain, w_router, shared_gate, shared_up, shared_down, expert_gate, expert_up, expert_down)))

    def wrapped(flat, *weights):
        return forward(flat, routes, weights)
    output, pullback = jax.vjp(wrapped, hidden_in.astype(jnp.float32), *params)
    grads = pullback(cotangent.astype(jnp.float32))
    return (output.astype(jnp.bfloat16), grads[0], grads[1], grads[2], grads[3], grads[4], grads[5], grads[6], grads[7], grads[8], grads[9], grads[10], grads[11], grads[12], grads[13])
```

```python
import functools

import jax
import jax.numpy as jnp
from jax import lax
from jax.sharding import PartitionSpec as P

HEADS = 12
HEAD_DIM = 64
BLOCK = 256
CHUNK = 256
ALL = ("expert", "fsdp")
EPSILON = 1e-06
BF = jnp.bfloat16
F32 = jnp.float32


def rope_tables(length, head_size):
    half = head_size // 2
    freqs = jnp.exp(-jnp.log(10000.0) * jnp.arange(half, dtype=F32) * 2.0 / head_size)
    angles = jnp.arange(length, dtype=F32)[:, None] * freqs[None, :]
    return (jnp.cos(angles)[:, None, :], jnp.sin(angles)[:, None, :])


def rotate(values, cosine, sine):
    half = values.shape[-1] // 2
    first = values[..., :half]
    second = values[..., half:]
    return jnp.concatenate(
        [first * cosine - second * sine, second * cosine + first * sine], axis=-1
    )


def dot(left, right, contract):
    return lax.dot_general(left, right, (contract, ((), ())), preferred_element_type=F32)


def mm(left, right):
    return dot(left, right, ((1,), (0,)))


def mm_tl(left, right):
    return dot(left, right, ((0,), (0,)))


def mm_tr(left, right):
    return dot(left, right, ((1,), (1,)))


def gated_backward(gate_part, up_part, grad):
    sig = jax.nn.sigmoid(gate_part)
    silu = gate_part * sig
    grad_gate = (grad * up_part * (sig * (1.0 + gate_part * (1.0 - sig)))).astype(BF)
    grad_up = (grad * silu).astype(BF)
    return grad_gate, grad_up


def norm_backward(values, scale, gain, grad):
    weighted = gain * grad
    inner = jnp.mean(weighted * values, axis=-1, keepdims=True)
    grad_values = scale * weighted - values * (scale * scale * scale) * inner
    return grad_values, jnp.sum(grad * values * scale, axis=0)


def to_chunks(block):
    rows, columns = block.shape
    return block.reshape(rows, columns // CHUNK, CHUNK).transpose(1, 0, 2).reshape(-1, CHUNK)


def from_chunks(gathered, rows, columns):
    parts = gathered.shape[0]
    return (
        gathered.reshape(parts, columns // CHUNK, rows, CHUNK)
        .transpose(0, 2, 1, 3)
        .reshape(parts * rows, columns)
    )


def split_chunks(full, parts):
    rows = full.shape[0] // parts
    columns = full.shape[1]
    return (
        full.reshape(parts, rows, columns // CHUNK, CHUNK)
        .transpose(0, 2, 1, 3)
        .reshape(parts, rows * columns // CHUNK, CHUNK)
    )


def gather_fsdp(block, n_f):
    if n_f != 4:
        return lax.all_gather(block, "fsdp", axis=0, tiled=True)
    rows = block.shape[0]
    own = lax.axis_index("fsdp")
    full = jnp.zeros((n_f * rows,) + block.shape[1:], block.dtype)
    full = lax.dynamic_update_slice(full, block, (own * rows, 0))
    for k in range(1, n_f):
        part = lax.ppermute(block, "fsdp", [(i, i ^ k) for i in range(n_f)])
        full = lax.dynamic_update_slice(full, part, ((own ^ k) * rows, 0))
    return full


def gather_expert(block, n_e):
    index = lax.axis_index("expert")
    height, core = index // 2, index % 2
    levels = n_e // 2
    line = jnp.zeros((levels,) + block.shape, block.dtype)
    line = lax.dynamic_update_slice(line, block[None], (height, 0, 0))
    for k in range(1, levels):
        part = lax.ppermute(block, "expert", [(i, i ^ (2 * k)) for i in range(n_e)])
        line = lax.dynamic_update_slice(line, part[None], (height ^ k, 0, 0))
    other = lax.ppermute(line, "expert", [(i, i ^ 1) for i in range(n_e)])
    full = jnp.zeros((levels, 2) + block.shape, block.dtype)
    full = lax.dynamic_update_slice(full, line[:, None], (0, core, 0, 0))
    full = lax.dynamic_update_slice(full, other[:, None], (0, 1 - core, 0, 0))
    return full.reshape((n_e,) + block.shape)


def attention_forward(query, key, value):
    length = query.shape[0]
    mixes, probs = [], []
    for start in range(0, length, BLOCK):
        stop = start + BLOCK
        scores = jnp.einsum(
            "qhd,khd->hqk", query[start:stop], key[:stop], preferred_element_type=F32
        ) * (HEAD_DIM**-0.5)
        exponent = jnp.exp(scores - jnp.max(scores, axis=-1, keepdims=True))
        prob = exponent / jnp.sum(exponent, axis=-1, keepdims=True)
        mix = jnp.einsum(
            "hqk,khd->qhd", prob.astype(BF), value[:stop], preferred_element_type=F32
        )
        mixes.append(mix.astype(BF).reshape(BLOCK, HEADS * HEAD_DIM))
        probs.append(prob)
    return jnp.concatenate(mixes, axis=0), probs


def attention_backward(query, key, value, grad_mix, probs):
    length = query.shape[0]
    scale = HEAD_DIM**-0.5
    grad_key = jnp.zeros(key.shape, F32)
    grad_value = jnp.zeros(value.shape, F32)
    grad_queries = []
    for index, start in enumerate(range(0, length, BLOCK)):
        stop = start + BLOCK
        prob = probs[index]
        grad_block = grad_mix[start:stop]
        grad_prob = jnp.einsum(
            "qhd,khd->hqk", grad_block, value[:stop], preferred_element_type=F32
        )
        grad_scores = (
            prob * (grad_prob - jnp.sum(prob * grad_prob, axis=-1, keepdims=True))
        ).astype(BF)
        grad_queries.append(
            jnp.einsum("hqk,khd->qhd", grad_scores, key[:stop], preferred_element_type=F32) * scale
        )
        dk = jnp.einsum(
            "hqk,qhd->khd", grad_scores, query[start:stop], preferred_element_type=F32
        )
        dv = jnp.einsum(
            "hqk,qhd->khd", prob.astype(BF), grad_block, preferred_element_type=F32
        )
        pad = ((0, length - stop), (0, 0), (0, 0))
        grad_key = grad_key + jnp.pad(dk * scale, pad)
        grad_value = grad_value + jnp.pad(dv, pad)
    return jnp.concatenate(grad_queries, axis=0), grad_key, grad_value


def per_device(
    hidden_in,
    routes,
    attn_gain,
    w_query,
    w_key,
    w_value,
    w_output,
    ffn_gain,
    w_router,
    shared_gate,
    shared_up,
    shared_down,
    expert_gate,
    expert_up,
    expert_down,
    cotangent,
    n_e,
    n_f,
):
    n_all = n_e * n_f
    tokens, width = hidden_in.shape
    rows = w_query.shape[0]
    n_experts = w_router.shape[1]
    hidden = shared_gate.shape[1]
    down_rows = shared_down.shape[0]
    capacity = 2 * 2 * tokens // n_experts

    extras = jnp.concatenate([attn_gain, ffn_gain, w_router.reshape(-1)])
    extras = jnp.pad(extras, (0, 8 * width - extras.shape[0])).reshape(8, width)
    first = lax.all_gather(
        jnp.concatenate([w_query, w_key, w_value, w_output, extras], axis=0), ALL, axis=0
    )
    w_q, w_k, w_v, w_o = (
        first[:, i * rows : (i + 1) * rows].reshape(n_all * rows, width) for i in range(4)
    )
    tail = first[:, 4 * rows]
    gain_one = tail[:, :rows].reshape(-1).astype(F32)
    gain_two = tail[:, rows : 2 * rows].reshape(-1).astype(F32)
    router = tail[:, 2 * rows : (2 + n_experts) * rows].reshape(n_all * rows, n_experts)

    second = lax.all_gather(
        jnp.concatenate([to_chunks(shared_gate), to_chunks(shared_up), to_chunks(shared_down)]),
        ALL,
        axis=0,
    )
    per = rows * hidden // CHUNK
    s_gate = from_chunks(second[:, :per], rows, hidden)
    s_up = from_chunks(second[:, per : 2 * per], rows, hidden)
    s_down = from_chunks(second[:, 2 * per :], down_rows, width)

    route_rows = jnp.pad(routes.T.astype(BF), ((0, 14), (0, width - tokens)))
    cot_all = gather_expert(jnp.concatenate([cotangent, route_rows], axis=0), n_e)
    e_gate = gather_fsdp(expert_gate[0], n_f)
    e_up = gather_fsdp(expert_up[0], n_f)
    e_down = gather_fsdp(expert_down[0], n_f)

    cosine, sine = rope_tables(tokens, HEAD_DIM)
    x = hidden_in.astype(F32)
    r1 = lax.rsqrt(jnp.mean(x * x, axis=-1, keepdims=True) + EPSILON)
    n1 = (x * r1 * gain_one).astype(BF)
    heads = (tokens, HEADS, HEAD_DIM)
    query = rotate(mm(n1, w_q).reshape(heads), cosine, sine).astype(BF)
    key = rotate(mm(n1, w_k).reshape(heads), cosine, sine).astype(BF)
    value = mm(n1, w_v).astype(BF).reshape(heads)
    mix, probs = attention_forward(query, key, value)
    h = x + mm(mix, w_o)
    r2 = lax.rsqrt(jnp.mean(h * h, axis=-1, keepdims=True) + EPSILON)
    n2 = (h * r2 * gain_two).astype(BF)

    n2_all = lax.all_gather(n2, "expert", axis=0)
    me = lax.axis_index("expert")
    routes_all = cot_all[:, tokens : tokens + 2, :tokens].astype(F32)
    mine = routes_all == me.astype(F32)
    mask = jnp.any(mine, axis=1)
    position = jnp.arange(tokens, dtype=jnp.int32)
    before = (position[:, None] < position[None, :]).astype(BF)
    rank = mm(mask.astype(BF), before)
    slot = jnp.arange(capacity, dtype=F32)
    pick = (mask[:, None, :] & (rank[:, None, :] == slot[None, :, None])).astype(BF)
    other = jnp.sum(routes_all, axis=1) - me.astype(F32)
    other_slot = jnp.einsum("skt,st->sk", pick, other.astype(BF), preferred_element_type=F32)

    def take(source):
        return (
            jnp.einsum("skt,std->skd", pick, source, preferred_element_type=F32)
            .astype(BF)
            .reshape(n_e * capacity, width)
        )

    def put(slots):
        return jnp.einsum(
            "skt,skd->std",
            pick,
            slots.reshape(n_e, capacity, width),
            preferred_element_type=F32,
        ).astype(BF)

    e_rows = take(n2_all)
    e_cot = take(cot_all[:, :tokens]).astype(F32)
    e_logits = mm(e_rows, router)
    expert_ids = jnp.arange(n_experts, dtype=F32)[None, :]
    e_diff = jnp.sum(
        jnp.where(expert_ids == me.astype(F32), e_logits, 0.0)
        - jnp.where(expert_ids == other_slot.reshape(-1, 1), e_logits, 0.0),
        axis=1,
        keepdims=True,
    )
    e_gates = jax.nn.sigmoid(e_diff)
    ge = mm(e_rows, e_gate)
    ue = mm(e_rows, e_up)
    inner = (ge * jax.nn.sigmoid(ge) * ue).astype(BF)
    result = mm(inner, e_down).astype(BF).astype(F32)
    c = (e_gates * e_cot).astype(BF)
    dge, due = gated_backward(ge, ue, mm_tr(c, e_down))
    b = (mm_tr(dge, e_gate) + mm_tr(due, e_up)).astype(BF)
    dgate_slot = jnp.sum(e_cot * result, axis=-1).reshape(n_e, 1, capacity)
    high = lax.reduce_precision(dgate_slot, 8, 7)
    low = (dgate_slot - high).astype(BF)
    pair = jnp.concatenate([high.astype(BF), low], axis=1)
    dgate_rows = jnp.einsum("sik,skt->sit", pair, pick, preferred_element_type=F32)
    dgate_rows = jnp.where(mine[:, :, None, :], dgate_rows[:, None], 0.0).astype(BF)
    dgate_rows = jnp.pad(
        dgate_rows.reshape(n_e, 4, tokens), ((0, 0), (0, 12), (0, width - tokens))
    )
    b_back = lax.psum_scatter(
        jnp.concatenate([put(b), dgate_rows], axis=1), "expert", scatter_dimension=0
    )
    y_back = lax.psum_scatter(
        put((e_gates * result).astype(BF)), "expert", scatter_dimension=0
    ).astype(F32)

    def reduce_fsdp(full):
        parts = full.astype(BF).reshape(n_f, full.shape[0] // n_f, full.shape[1])
        parts = lax.all_to_all(parts, "fsdp", split_axis=0, concat_axis=0, tiled=True)
        return jnp.sum(parts.astype(F32), axis=0)[None]

    grad_e_down = reduce_fsdp(mm_tl(inner, c))
    grad_e_gate = reduce_fsdp(mm_tl(e_rows, dge))
    grad_e_up = reduce_fsdp(mm_tl(e_rows, due))

    sg = mm(n2, s_gate)
    su = mm(n2, s_up)
    sh = (sg * jax.nn.sigmoid(sg) * su).astype(BF)
    shared_result = mm(sh, s_down)
    gy = cotangent.astype(F32)
    dsg, dsu = gated_backward(sg, su, mm_tr(cotangent, s_down))
    shared_grads = lax.psum_scatter(
        jnp.concatenate(
            [
                split_chunks(mm_tl(n2, dsg).astype(BF), n_all),
                split_chunks(mm_tl(n2, dsu).astype(BF), n_all),
                split_chunks(mm_tl(sh, cotangent).astype(BF), n_all),
            ],
            axis=1,
        ),
        ALL,
        scatter_dimension=0,
    ).astype(F32)
    grad_s_gate = from_chunks(shared_grads[None, :per], rows, hidden)
    grad_s_up = from_chunks(shared_grads[None, per : 2 * per], rows, hidden)
    grad_s_down = from_chunks(shared_grads[None, 2 * per :], down_rows, width)
    output = (h + y_back + shared_result).astype(BF)

    logits = mm(n2, router)
    ids = jnp.arange(n_experts, dtype=jnp.int32)
    onehot = (routes[:, :, None] == ids).astype(F32)
    chosen = jnp.sum(logits[:, None, :] * onehot, axis=-1)
    gates = jax.nn.softmax(chosen, axis=-1)
    returned = b_back[tokens : tokens + 4, :tokens].astype(F32)
    dgate = (returned[0::2] + returned[1::2]).T
    dchosen = gates * (dgate - jnp.sum(gates * dgate, axis=-1, keepdims=True))
    dlogits = jnp.sum(dchosen[:, :, None] * onehot, axis=1).astype(BF)
    grad_router = mm_tl(n2, dlogits)
    dn2 = (
        mm_tr(dsg, s_gate)
        + mm_tr(dsu, s_up)
        + mm_tr(dlogits, router)
        + b_back[:tokens].astype(F32)
    )
    grad_h, grad_gain_two = norm_backward(h, r2, gain_two, dn2)
    dh = gy + grad_h

    da = dh.astype(BF)
    grad_w_o = mm_tl(mix, da)
    grad_mix = mm_tr(da, w_o).astype(BF).reshape(heads)
    dqr, dkr, dvv = attention_backward(query, key, value, grad_mix, probs)
    dq = rotate(dqr, cosine, -sine).astype(BF).reshape(tokens, width)
    dk = rotate(dkr, cosine, -sine).astype(BF).reshape(tokens, width)
    dv = dvv.astype(BF).reshape(tokens, width)
    dn1 = mm_tr(dq, w_q) + mm_tr(dk, w_k) + mm_tr(dv, w_v)
    grad_x, grad_gain_one = norm_backward(x, r1, gain_one, dn1)
    grad_hidden = dh + grad_x

    small = jnp.concatenate(
        [
            grad_gain_one.reshape(n_all, rows),
            grad_gain_two.reshape(n_all, rows),
            grad_router.reshape(n_all, rows * n_experts),
        ],
        axis=1,
    )
    small = jnp.pad(small, ((0, 0), (0, 8 * width - small.shape[1]))).reshape(n_all, 8, width)
    dense = [mm_tl(n1, dq), mm_tl(n1, dk), mm_tl(n1, dv), grad_w_o]
    dense = [item.reshape(n_all, rows, width) for item in dense] + [small]
    dense = lax.psum_scatter(
        jnp.concatenate([item.astype(BF) for item in dense], axis=1), ALL, scatter_dimension=0
    ).astype(F32)
    last = dense[4 * rows]
    return (
        output,
        grad_hidden,
        last[:rows],
        dense[:rows],
        dense[rows : 2 * rows],
        dense[2 * rows : 3 * rows],
        dense[3 * rows : 4 * rows],
        last[rows : 2 * rows],
        last[2 * rows : (2 + n_experts) * rows].reshape(rows, n_experts),
        grad_s_gate,
        grad_s_up,
        grad_s_down,
        grad_e_gate,
        grad_e_up,
        grad_e_down,
    )


def solution(mesh):
    row = P(ALL, None)
    vector = P(ALL)
    expert = P("expert", "fsdp", None)
    return jax.shard_map(
        functools.partial(per_device, n_e=mesh.shape["expert"], n_f=mesh.shape["fsdp"]),
        mesh=mesh,
        in_specs=(
            (row, row, vector, row, row, row, row, vector)
            + (row, row, row, row, expert, expert, expert, row)
        ),
        out_specs=(
            (row, row, vector, row, row, row, row, vector)
            + (row, row, row, row, expert, expert, expert)
        ),
        check_vma=False,
    )
```
